32 devices in a mesh: pole: 2 (over x), wide: 8 (over z, y), narrow: 2 (over core).
Axes of the slice: x: 2, y: 2, z: 4, core: 2. Of those that a mesh axis runs over, the one named last changes fastest.
Arguments:
- h_panel: float32 [512, 2048], P(('pole', 'wide', 'narrow')), parts along dimension 0, may hold values from -0.3 to 0.3
- s_panel: float32 [512, 2048], P(('pole', 'wide', 'narrow')), parts along dimension 0, may hold values from -0.3 to 0.3
- col_index: int32 [512], P('pole'), parts along dimension 0, may hold values from 0 to 255, each once
- pattern: int32 [256], P(('pole', 'wide', 'narrow')), parts along dimension 0, may hold values 0 or 1
- dinv: float32 [512, 256], P('pole'), parts along dimension 0, may hold values from -4 to 4, as said below
- ainv_cc: float32 [4096, 8, 2, 128], P(('pole', 'wide'), None, 'narrow'), parts along dimension 0, may hold values from -1 to 1
Outputs:
- ainv_ck: float32 [4096, 256], P(('pole', 'wide'), 'narrow'), parts along dimension 0
- ainv_kk: float32 [512, 256], P(('pole', 'wide'), 'narrow'), parts along dimension 0
The draws below stay inside these ranges and needn't reach their ends.
There are 2 independent parts, one for each index of `pole`. The reference program is written for one: setup_inputs(seed, part) draws one part's arguments, and reference() takes and returns one part's arrays. A program takes and returns all parts, laid end to end along the dimension named above; each array names one. Nothing has to cross between parts.
Inputs may be any that keep to these rules, and one draw needn't show every extreme that they name: `dinv`: diagonal entries between 0.25 and 4, off-diagonal entries at most 4 / sqrt(256) in magnitude.
All inputs are finite; a program needn't handle non-finite values. No bound on the sum of `pattern` on one device may be relied on, other than what follows from the above.
Results may differ from the reference program's by a relative error of at most 0.00011.
Values sent between devices are 32-bit elements; how exact they have to be, the bound alone decides.
No kernel may reach another device: no remote copies, remote signals or barrier semaphores. Data moves between devices by JAX's collectives and lax.ppermute only.
A program may use at most 64 MiB of HBM per device.

```python
import math
import jax
import jax.numpy as jnp
from jax import lax

B = 256
UNIT = 128
PATTERN_ROWS = 16
NCR = 2048
N_WIDE = 8
N_NARROW = 2


def draw_dinv(key, part):
    first, second = jax.random.split(key, 2)
    diagonal = jnp.exp(jax.random.uniform(first, (B,), jnp.float32, math.log(0.5), math.log(2.0)))
    spread = jnp.clip(jax.random.normal(second, (B, B), jnp.float32), -4.0, 4.0) * (0.5 / math.sqrt(B))
    matrix = spread + jnp.diag(diagonal)
    return matrix


def touch_ends(result, stream_key, least, largest):
    longest = result.shape.index(max(result.shape))
    spots = []
    for shift in (0, 1):
        where = [jax.random.randint(jax.random.fold_in(stream_key, axis), (), 0, length) for axis, length in enumerate(result.shape)]
        where[longest] = (where[longest] + shift) % result.shape[longest]
        spots.append(tuple(where))
    return result.at[spots[0]].set(least).at[spots[1]].set(largest)


def block_levels(own_key, shape, cuts, low, largest):
    loudness = 1.0
    for axis_at, parts in cuts:
        steps = jax.random.uniform(jax.random.fold_in(jax.random.fold_in(own_key, 6), axis_at), (parts,), jnp.float32, low / len(cuts), largest / len(cuts))
        loudness = loudness * jnp.repeat(jnp.exp(steps), shape[axis_at] // parts).reshape((-1,) + (1,) * (len(shape) - 1 - axis_at))
    return loudness


def normal_values(key, shape, deviation, bound, cuts=(), held_as=jnp.bfloat16):
    entries = deviation * jax.random.normal(key, shape, jnp.float32)
    if cuts:
        entries = entries * block_levels(key, shape, cuts, -0.22, 0.18)
    return jnp.clip(entries, -bound, bound).astype(held_as)


def setup_inputs(seed: int = 0, part: int = 0) -> dict:
    arg_keys = jax.random.split(jax.random.key(seed), 7)
    part_splits = jax.random.split(jax.random.fold_in(arg_keys[6], part), 7)
    return {
        "h_panel": normal_values(part_splits[0], (B, NCR), 0.05, 0.3, ((0, 16),), jnp.float32),
        "s_panel": normal_values(part_splits[1], (B, NCR), 0.05, 0.3, ((0, 16),), jnp.float32),
        "col_index": jax.random.permutation(part_splits[2], B).astype(jnp.int32),
        "pattern": touch_ends((jax.random.randint(part_splits[3], (NCR // PATTERN_ROWS,), 0, 4) < 3).astype(jnp.int32), jax.random.fold_in(part_splits[3], 1), 0, 1),
        "dinv": draw_dinv(jax.random.fold_in(jax.random.fold_in(arg_keys[6], part), 71), part),
        "ainv_cc": normal_values(part_splits[5], (NCR, N_WIDE, N_NARROW, UNIT), (2 * UNIT * N_WIDE // 64) ** -0.5, 1.0, ((0, 8), (2, 2)), jnp.float32),
    }


POLE_SHIFT = 0.5


def reference(h_panel, s_panel, col_index, pattern, dinv, ainv_cc):
    panel_cols = h_panel - POLE_SHIFT * s_panel
    rows_total = panel_cols.shape[1]
    placed = jnp.zeros((rows_total, B), jnp.float32).at[:, col_index].set(panel_cols.T)
    live_rows = jnp.repeat((pattern > 0).astype(jnp.float32), PATTERN_ROWS)
    placed = placed * live_rows[:, None]
    factor_panel = jnp.dot(placed, dinv, precision=lax.Precision.HIGHEST, preferred_element_type=jnp.float32)
    inverse_flat = ainv_cc.reshape(rows_total, rows_total)
    ainv_ck = -jnp.dot(inverse_flat, factor_panel, precision=lax.Precision.HIGHEST, preferred_element_type=jnp.float32)
    ainv_kk = dinv - jnp.dot(factor_panel.T, ainv_ck, precision=lax.Precision.HIGHEST, preferred_element_type=jnp.float32)
    return ainv_ck, ainv_kk
```

```python
import functools

import jax
import jax.numpy as jnp
from jax import lax
from jax.experimental import pallas as pl
from jax.experimental.pallas import tpu as pltpu
from jax.sharding import PartitionSpec as P

POLE_SHIFT = 0.5
LANES = 128
SUBLANES = 8
VMEM = pl.BlockSpec(memory_space=pltpu.VMEM)
SMEM = pl.BlockSpec(memory_space=pltpu.SMEM)


def split(x):
    high = x.astype(jnp.bfloat16)
    return high, (x - high.astype(jnp.float32)).astype(jnp.bfloat16)


def dot3(a, b, dims):
    one = functools.partial(
        lax.dot_general, dimension_numbers=(dims, ((), ())), preferred_element_type=jnp.float32
    )
    return one(a[0], b[0]) + (one(a[0], b[1]) + one(a[1], b[0]))


def call(kernel, outs, in_specs, args, flops, **more):
    shapes = [jax.ShapeDtypeStruct(*o) for o in outs]
    size = sum(x.size * x.dtype.itemsize for x in (*args, *shapes))
    return pl.pallas_call(
        kernel,
        out_shape=shapes,
        in_specs=in_specs,
        out_specs=[VMEM] * len(shapes),
        cost_estimate=pl.CostEstimate(flops=flops, bytes_accessed=size, transcendentals=0),
        **more,
    )(*args)


def prep_kernel(where, pattern, h, s, own, other, mask):
    core = where[1]
    columns = h.shape[0]
    bands = own.shape[0] // (h.shape[1] // (2 * LANES))
    blocks = own.shape[0] // bands
    for band in range(bands):
        low, high = band * SUBLANES, min(columns, (band + 1) * SUBLANES)
        for block in range(blocks):
            for out, half in ((own, core), (other, 1 - core)):
                at = pl.ds(pl.multiple_of((2 * block + half) * LANES, LANES), LANES)
                tile = h[low:high, at] - POLE_SHIFT * s[low:high, at]
                if high - low < SUBLANES:
                    tile = jnp.concatenate(
                        [tile, jnp.zeros((SUBLANES - high + low, LANES), jnp.float32)]
                    )
                out[band * blocks + block] = tile
    groups = pattern.shape[0]
    group = lax.broadcasted_iota(jnp.int32, (SUBLANES, LANES), 1) // (LANES // groups)
    live = jnp.zeros((SUBLANES, LANES), jnp.float32)
    for g in range(groups):
        live = jnp.where(group == g, (pattern[g] > 0).astype(jnp.float32), live)
    mask[0] = live


def ready_kernel(where, index, dinv, m, d_high, d_low, m_high, m_low):
    core = where[1]
    total, width = index.shape[0], dinv.shape[1]
    picked = (lax.broadcasted_iota(jnp.int32, (total, width), 1) == index[...]).astype(jnp.float32)
    half = width // 2
    for j, part in enumerate((core, 1 - core)):
        at = pl.ds(pl.multiple_of(part * half, LANES), half)
        rows = lax.dot_general(
            picked,
            dinv[:, at],
            (((1,), (0,)), ((), ())),
            precision=lax.Precision.HIGHEST,
            preferred_element_type=jnp.float32,
        )
        high, low = split(rows)
        d_high[:, j * half : (j + 1) * half] = high
        d_low[:, j * half : (j + 1) * half] = low
    for block in range(m.shape[1]):
        high, low = split(m[:, block, :])
        m_high[:, block * LANES : (block + 1) * LANES] = high
        m_low[:, block * LANES : (block + 1) * LANES] = low


def factor_kernel(count, where, d_high, d_low, *refs):
    parts, out = refs[:count], refs[count]
    chip, core = where[0], where[1]
    blocks = where.shape[0] - 2
    bands = (parts[0].shape[0] - 1) // blocks
    rows = jnp.concatenate([p[band * blocks + chip] for p in parts for band in range(bands)])
    rows = rows * parts[0][bands * blocks][:1, :]
    value = dot3((d_high[...], d_low[...]), split(rows), ((0,), (0,)))
    half = value.shape[0] // 2
    out[pl.ds(pl.multiple_of(core * half, SUBLANES), half), :] = value[:half]
    out[pl.ds(pl.multiple_of((1 - core) * half, SUBLANES), half), :] = value[half:]


def product_kernel(count, where, d_high, d_low, m_high, m_low, *refs):
    parts, (keep, send, live, p_high, p_low) = refs[:count], refs[count:]
    blocks = where.shape[0] - 2
    bands = (parts[0].shape[0] - 1) // blocks
    for k, part in enumerate(parts):
        live[pl.ds(where[2 + k], 1), :] = part[bands * blocks][:1, :]
    deep = bands * SUBLANES
    for block in range(blocks):
        row = live[block : block + 1, :]
        at = slice(block * LANES, (block + 1) * LANES)
        for k, part in enumerate(parts):
            rows = jnp.concatenate([part[band * blocks + block] for band in range(bands)]) * row
            high, low = split(rows)
            p_high[k * deep : (k + 1) * deep, at] = high
            p_low[k * deep : (k + 1) * deep, at] = low
    first = dot3((m_high[...], m_low[...]), (p_high[...], p_low[...]), ((1,), (1,)))
    both = dot3(split(first), (d_high[...], d_low[...]), ((1,), (0,)))
    half = both.shape[1] // 2
    keep[...] = both[:, :half]
    send[...] = both[:, half:]


def corner_kernel(where, keep, received, factor, factor_other, out, term):
    core = where[1]
    out[...] = -(keep[...] + received[...])
    half = out.shape[0] // 2
    for j, part in enumerate((core, 1 - core)):
        rows = out[pl.ds(pl.multiple_of(part * half, SUBLANES), half), :]
        value = dot3(split((factor, factor_other)[j][...]), split(rows), ((1,), (0,)))
        if j == 0:
            term[...] = value
        else:
            term[...] += value


def local(wides, h_panel, s_panel, col_index, pattern, dinv, ainv_cc):
    columns = h_panel.shape[0]
    rows_here, blocks, _, unit = ainv_cc.shape
    width = dinv.shape[0]
    deep = -(-columns // SUBLANES) * SUBLANES
    tiles = deep // SUBLANES * blocks
    wide, narrow = lax.axis_index("wide"), lax.axis_index("narrow")
    swap = [(0, 1), (1, 0)]

    ring = list(range(0, wides, 2)) + list(range(1, wides, 2))[::-1]
    place = [ring.index(i) for i in range(wides)]
    ahead = [(ring[i], ring[(i + 1) % wides]) for i in range(wides)]
    back = [(b, a) for a, b in ahead]
    offsets = [0]
    for step in range(1, (wides + 1) // 2):
        offsets += [-step, step]
    if wides % 2 == 0:
        offsets.append(-(wides // 2))
    table = jnp.array([[ring[(place[i] + o) % wides] for o in offsets] for i in range(wides)], jnp.int32)
    chips = lax.dynamic_index_in_dim(table, wide, 0, keepdims=False)
    where = jnp.concatenate([jnp.stack([wide, narrow]).astype(jnp.int32), chips])

    cuts = [(tiles, SUBLANES, LANES)] * 2 + [(1, SUBLANES, LANES)]
    own, other, mask = call(
        prep_kernel,
        [(c, jnp.float32) for c in cuts],
        [SMEM, SMEM, VMEM, VMEM],
        (where, pattern, h_panel, s_panel),
        2 * h_panel.size,
    )
    mine = jnp.concatenate([own, lax.ppermute(other, "narrow", swap), mask])

    parts = [mine]
    up = down = mine
    for step in range(1, (wides + 1) // 2):
        up = lax.ppermute(up, "wide", ahead)
        down = lax.ppermute(down, "wide", back)
        parts += [up, down]
    if wides % 2 == 0:
        parts.append(lax.ppermute(up, "wide", ahead))

    index = jnp.take(col_index.reshape(wides, 2, columns), chips, axis=0)
    index = jnp.where(narrow == 0, index, index[:, ::-1])
    index = jnp.pad(index, ((0, 0), (0, 0), (0, deep - columns))).reshape(-1, 1)
    total = index.shape[0]
    d_high, d_low, m_high, m_low = call(
        ready_kernel,
        [((total, width), jnp.bfloat16)] * 2 + [((rows_here, blocks * unit), jnp.bfloat16)] * 2,
        [SMEM, VMEM, VMEM, VMEM],
        (where, index, dinv, ainv_cc.reshape(rows_here, blocks, unit)),
        12 * total * width * width,
    )

    factor = call(
        functools.partial(factor_kernel, wides),
        [((width, unit), jnp.float32)],
        [SMEM] + [VMEM] * (2 + wides),
        (where, d_high, d_low, *parts),
        6 * total * width * unit,
    )[0]
    factor_other = lax.ppermute(factor, "narrow", swap)
    keep, send = call(
        functools.partial(product_kernel, wides),
        [((rows_here, width // 2), jnp.float32)] * 2,
        [SMEM] + [VMEM] * (4 + wides),
        (where, d_high, d_low, m_high, m_low, *parts),
        6 * total * rows_here * (blocks * unit + width),
        scratch_shapes=[pltpu.VMEM((blocks, unit), jnp.float32)]
        + [pltpu.VMEM((total, blocks * unit), jnp.bfloat16)] * 2,
    )
    received = lax.ppermute(send, "narrow", swap)
    ainv_ck, term = call(
        corner_kernel,
        [((rows_here, width // 2), jnp.float32), ((width, width // 2), jnp.float32)],
        [SMEM] + [VMEM] * 4,
        (where, keep, received, factor, factor_other),
        6 * width * width * rows_here,
    )
    share = width // wides
    shares = lax.all_to_all(term.reshape(wides, share, -1), "wide", 0, 0, tiled=True)
    corner = lax.dynamic_slice(dinv, (wide * share, narrow * (width // 2)), (share, width // 2))
    return ainv_ck, corner - jnp.sum(shares, axis=0)


def solution(mesh):
    placed = (
        P(("pole", "wide", "narrow"), None),
        P(("pole", "wide", "narrow"), None),
        P("pole"),
        P(("pole", "wide", "narrow")),
        P("pole", None),
        P(("pole", "wide"), None, "narrow", None),
    )
    return jax.shard_map(
        functools.partial(local, mesh.shape["wide"]),
        mesh=mesh,
        in_specs=placed,
        out_specs=(P(("pole", "wide"), "narrow"), P(("pole", "wide"), "narrow")),
        check_vma=False,
    )
```

```python
import functools

import jax
import jax.numpy as jnp
from jax import lax
from jax.experimental import pallas as pl
from jax.experimental.pallas import tpu as pltpu
from jax.sharding import PartitionSpec as P

POLE_SHIFT = 0.5
LANES = 128
SUBLANES = 8
VMEM_LIMIT = 24 * 2**20
VMEM = pl.BlockSpec(memory_space=pltpu.VMEM)
HBM = pl.BlockSpec(memory_space=pltpu.HBM)


def split(x):
    high = x.astype(jnp.bfloat16)
    return high, (x - high.astype(jnp.float32)).astype(jnp.bfloat16)


def dot3(a, b, dims):
    one = functools.partial(
        lax.dot_general, dimension_numbers=(dims, ((), ())), preferred_element_type=jnp.float32
    )
    return one(a[0], b[0]) + (one(a[0], b[1]) + one(a[1], b[0]))


def call(kernel, outs, in_specs, args, flops, scratch=()):
    shapes = [jax.ShapeDtypeStruct(*o) for o in outs]
    size = sum(x.size * x.dtype.itemsize for x in (*args, *shapes))
    return pl.pallas_call(
        kernel,
        out_shape=shapes,
        in_specs=in_specs,
        out_specs=[VMEM] * len(shapes),
        scratch_shapes=scratch,
        cost_estimate=pl.CostEstimate(flops=flops, bytes_accessed=size, transcendentals=0),
        compiler_params=pltpu.CompilerParams(vmem_limit_bytes=VMEM_LIMIT),
    )(*args)


def in_hbm(x):
    return pltpu.with_memory_space_constraint(x, pltpu.HBM)


def chip_at(place, wides):
    return jnp.where(place < (wides + 1) // 2, 2 * place, 2 * (wides - 1 - place) + 1)


def place_of(chip, wides):
    return jnp.where(chip % 2 == 0, chip // 2, wides - 1 - chip // 2)


def offsets(wides):
    found = [0]
    for step in range(1, (wides + 1) // 2):
        found += [-step, step]
    if wides % 2 == 0:
        found.append(-(wides // 2))
    return found


def prep_kernel(pattern, h, s, own, other, flags, h_here, s_here, flag_sem, sems):
    core = lax.axis_index("narrow")
    columns = h.shape[0]
    tiles = other.shape[0]
    blocks = h.shape[1] // (2 * LANES)
    bands = tiles // blocks
    reads = []
    for band in range(bands):
        at = pl.ds(band * SUBLANES, min(columns - band * SUBLANES, SUBLANES))
        reads.append(
            [
                pltpu.make_async_copy(a.at[at], b.at[at], sems.at[i, band])
                for i, (a, b) in enumerate(((h, h_here), (s, s_here)))
            ]
        )
    live_read = pltpu.make_async_copy(pattern, flags, flag_sem)
    for pair in reads:
        for read in pair:
            read.start()
    live_read.start()
    for band in range(bands):
        for read in reads[band]:
            read.wait()
        low, high = band * SUBLANES, min(columns, (band + 1) * SUBLANES)
        for out, half in ((other, 1 - core), (own, core)):
            for block in range(blocks):
                at = pl.ds(pl.multiple_of((2 * block + half) * LANES, LANES), LANES)
                tile = h_here[low:high, at] - POLE_SHIFT * s_here[low:high, at]
                if high - low < SUBLANES:
                    rest = jnp.zeros((SUBLANES - high + low, LANES), jnp.float32)
                    tile = jnp.concatenate([tile, rest])
                out[band * blocks + block] = tile
    live_read.wait()
    groups = pattern.shape[0]
    group = lax.broadcasted_iota(jnp.int32, (SUBLANES, LANES), 1) // (LANES // groups)
    live = jnp.zeros((SUBLANES, LANES), jnp.float32)
    for g in range(groups):
        live = jnp.where(group == g, (flags[g] > 0).astype(jnp.float32), live)
    own[2 * tiles] = live


def inverse_kernel(m, high, low, here, sems):
    reads = [
        pltpu.make_async_copy(m.at[:, b, :], here.at[:, pl.ds(b * LANES, LANES)], sems.at[b])
        for b in range(m.shape[1])
    ]
    for read in reads:
        read.start()
    for b, read in enumerate(reads):
        read.wait()
        at = slice(b * LANES, (b + 1) * LANES)
        high[:, at], low[:, at] = split(here[:, at])


def pivot_kernel(wides, index, dinv, high, low, high_t, low_t, picked):
    core, place = lax.axis_index("narrow"), place_of(lax.axis_index("wide"), wides)
    total, width = picked.shape
    deep = total // (2 * wides)
    lane = lax.broadcasted_iota(jnp.int32, (deep, width), 1)
    for k, offset in enumerate(offsets(wides)):
        chip = chip_at((place + offset + wides) % wides, wides)
        for j, part in enumerate((core, 1 - core)):
            rows = index[pl.ds(pl.multiple_of((2 * chip + part) * deep, SUBLANES), deep), :]
            at = (2 * k + j) * deep
            picked[at : at + deep, :] = (lane == rows).astype(jnp.float32)
    half = width // 2
    chosen = picked[...].astype(jnp.bfloat16)
    for piece, out, out_t in zip(split(dinv[...]), (high, low), (high_t, low_t)):
        rows = jnp.dot(chosen, piece, preferred_element_type=jnp.float32)
        out_t[...] = rows.T.astype(jnp.bfloat16)
        rows = rows.astype(jnp.bfloat16)

        @pl.when(core == 0)
        def _():
            out[...] = rows

        @pl.when(core != 0)
        def _():
            out[:, :half] = rows[:, half:]
            out[:, half:] = rows[:, :half]


def factor_kernel(wides, high_t, low_t, *refs):
    parts, out = refs[:wides], refs[wides]
    chip = lax.axis_index("wide")
    bands = (parts[0].shape[0] - 1) // wides
    rows = jnp.concatenate([p[band * wides + chip] for p in parts for band in range(bands)])
    rows = rows * parts[0][bands * wides][:1, :]
    out[...] = dot3((high_t[...], low_t[...]), split(rows), ((1,), (0,)))


def product_kernel(wides, d_high, d_low, m_high, m_low, *refs):
    parts, (keep, send, live, p_high, p_low) = refs[:wides], refs[wides:]
    place = place_of(lax.axis_index("wide"), wides)
    bands = (parts[0].shape[0] - 1) // wides
    for part, offset in zip(parts, offsets(wides)):
        chip = chip_at((place + offset + wides) % wides, wides)
        live[pl.ds(chip, 1), :] = part[bands * wides][:1, :]
    deep = bands * SUBLANES
    for block in range(wides):
        row = live[block : block + 1, :]
        at = slice(block * LANES, (block + 1) * LANES)
        for k, part in enumerate(parts):
            rows = jnp.concatenate([part[band * wides + block] for band in range(bands)]) * row
            high, low = split(rows)
            p_high[k * deep : (k + 1) * deep, at] = high
            p_low[k * deep : (k + 1) * deep, at] = low
    first = dot3((m_high[...], m_low[...]), (p_high[...], p_low[...]), ((1,), (1,)))
    both = dot3(split(first), (d_high[...], d_low[...]), ((1,), (0,)))
    half = both.shape[1] // 2
    keep[...] = both[:, :half]
    send[...] = both[:, half:]


def corner_kernel(keep, received, factor, factor_other, term):
    core = lax.axis_index("narrow")
    half = keep.shape[0] // 2
    value = None
    for from_here, part in ((factor, core), (factor_other, 1 - core)):
        at = pl.ds(pl.multiple_of(part * half, SUBLANES), half)
        more = dot3(split(from_here[...]), split(keep[at, :] + received[at, :]), ((1,), (0,)))
        value = more if value is None else value + more
    term[...] = value


def local(wides, h_panel, s_panel, col_index, pattern, dinv, ainv_cc):
    columns, rows_all = h_panel.shape
    rows_here, blocks, _, unit = ainv_cc.shape
    width = dinv.shape[0]
    deep = -(-columns // SUBLANES) * SUBLANES
    tiles = deep // SUBLANES * blocks
    total = 2 * wides * deep
    wide, narrow = lax.axis_index("wide"), lax.axis_index("narrow")
    swap = [(0, 1), (1, 0)]
    f32, bf16 = jnp.float32, jnp.bfloat16
    ring = [*range(0, wides, 2), *range(1, wides, 2)[::-1]]
    ahead = [(ring[i], ring[(i + 1) % wides]) for i in range(wides)]
    back = [(b, a) for a, b in ahead]

    own, other = call(
        prep_kernel,
        [((2 * tiles + 1, SUBLANES, LANES), f32), ((tiles, SUBLANES, LANES), f32)],
        [HBM] * 3,
        tuple(in_hbm(x) for x in (pattern, h_panel, s_panel)),
        2 * h_panel.size,
        [
            pltpu.SMEM(pattern.shape, jnp.int32),
            pltpu.VMEM(h_panel.shape, f32),
            pltpu.VMEM(h_panel.shape, f32),
            pltpu.SemaphoreType.DMA(()),
            pltpu.SemaphoreType.DMA((2, deep // SUBLANES)),
        ],
    )
    mine = lax.dynamic_update_slice(own, lax.ppermute(other, "narrow", swap), (tiles, 0, 0))

    parts = [mine]
    up = down = mine
    for step in range(1, (wides + 1) // 2):
        up = lax.ppermute(up, "wide", ahead)
        down = lax.ppermute(down, "wide", back)
        parts += [up, down]
    if wides % 2 == 0:
        parts.append(lax.ppermute(up, "wide", ahead))

    m_high, m_low = call(
        inverse_kernel,
        [((rows_here, blocks * unit), bf16)] * 2,
        [HBM],
        (in_hbm(ainv_cc.reshape(rows_here, blocks, unit)),),
        4 * ainv_cc.size,
        [pltpu.VMEM((rows_here, blocks * unit), f32), pltpu.SemaphoreType.DMA((blocks,))],
    )
    index = jnp.pad(col_index.reshape(-1, columns), ((0, 0), (0, deep - columns))).reshape(-1, 1)
    d_high, d_low, d_high_t, d_low_t = call(
        functools.partial(pivot_kernel, wides),
        [((total, width), bf16)] * 2 + [((width, total), bf16)] * 2,
        [VMEM] * 2,
        (index, dinv),
        4 * total * width * width,
        [pltpu.VMEM((total, width), f32)],
    )
    factor = call(
        functools.partial(factor_kernel, wides),
        [((width, unit), f32)],
        [VMEM] * (2 + wides),
        (d_high_t, d_low_t, *parts),
        6 * total * width * unit,
    )[0]
    factor_other = lax.ppermute(factor, "narrow", swap)
    keep, send = call(
        functools.partial(product_kernel, wides),
        [((rows_here, width // 2), f32)] * 2,
        [VMEM] * (4 + wides),
        (d_high, d_low, m_high, m_low, *parts),
        6 * total * rows_here * (blocks * unit + width),
        [pltpu.VMEM((blocks, unit), f32)] + [pltpu.VMEM((total, blocks * unit), bf16)] * 2,
    )
    received = lax.ppermute(send, "narrow", swap)
    term = call(
        corner_kernel,
        [((width, width // 2), f32)],
        [VMEM] * 4,
        (keep, received, factor, factor_other),
        6 * width * width * rows_here,
    )[0]
    share = width // wides
    shares = lax.all_to_all(term.reshape(wides, share, -1), "wide", 0, 0, tiled=True)
    corner = lax.dynamic_slice(dinv, (wide * share, narrow * (width // 2)), (share, width // 2))
    return -(keep + received), corner + jnp.sum(shares, axis=0)


def solution(mesh):
    placed = (
        P(("pole", "wide", "narrow"), None),
        P(("pole", "wide", "narrow"), None),
        P("pole"),
        P(("pole", "wide", "narrow")),
        P("pole", None),
        P(("pole", "wide"), None, "narrow", None),
    )
    return jax.shard_map(
        functools.partial(local, mesh.shape["wide"]),
        mesh=mesh,
        in_specs=placed,
        out_specs=(P(("pole", "wide"), "narrow"), P(("pole", "wide"), "narrow")),
        check_vma=False,
    )
```

```python
import functools

import jax
import jax.numpy as jnp
from jax import lax
from jax.experimental import pallas as pl
from jax.experimental.pallas import tpu as pltpu
from jax.sharding import PartitionSpec as P

POLE_SHIFT = 0.5
LANES = 128
SUBLANES = 8
VMEM_LIMIT = 24 * 2**20
VMEM = pl.BlockSpec(memory_space=pltpu.VMEM)
HBM = pl.BlockSpec(memory_space=pltpu.HBM)


def split(x):
    high = x.astype(jnp.bfloat16)
    return high, (x - high.astype(jnp.float32)).astype(jnp.bfloat16)


def dot3(a, b, dims):
    one = functools.partial(
        lax.dot_general, dimension_numbers=(dims, ((), ())), preferred_element_type=jnp.float32
    )
    return one(a[0], b[0]) + (one(a[0], b[1]) + one(a[1], b[0]))


def call(kernel, outs, in_specs, args, flops, scratch=()):
    shapes = [jax.ShapeDtypeStruct(*o) for o in outs]
    size = sum(x.size * x.dtype.itemsize for x in (*args, *shapes))
    return pl.pallas_call(
        kernel,
        out_shape=shapes,
        in_specs=in_specs,
        out_specs=[VMEM] * len(shapes),
        scratch_shapes=scratch,
        cost_estimate=pl.CostEstimate(flops=flops, bytes_accessed=size, transcendentals=0),
        compiler_params=pltpu.CompilerParams(vmem_limit_bytes=VMEM_LIMIT),
    )(*args)


def in_hbm(x):
    return pltpu.with_memory_space_constraint(x, pltpu.HBM)


def chip_at(place, wides):
    return jnp.where(place < (wides + 1) // 2, 2 * place, 2 * (wides - 1 - place) + 1)


def place_of(chip, wides):
    return jnp.where(chip % 2 == 0, chip // 2, wides - 1 - chip // 2)


def offsets(wides):
    found = [0]
    for step in range(1, (wides + 1) // 2):
        found += [-step, step]
    if wides % 2 == 0:
        found.append(-(wides // 2))
    return found


def prep_kernel(pattern, h, s, own, other, flags, h_here, s_here, flag_sem, sems):
    core = lax.axis_index("narrow")
    columns = h.shape[0]
    tiles = other.shape[0]
    blocks = h.shape[1] // (2 * LANES)
    bands = tiles // blocks
    reads = []
    for band in range(bands):
        at = pl.ds(band * SUBLANES, min(columns - band * SUBLANES, SUBLANES))
        reads.append(
            [
                pltpu.make_async_copy(a.at[at], b.at[at], sems.at[i, band])
                for i, (a, b) in enumerate(((h, h_here), (s, s_here)))
            ]
        )
    live_read = pltpu.make_async_copy(pattern, flags, flag_sem)
    for pair in reads:
        for read in pair:
            read.start()
    live_read.start()
    for band in range(bands):
        for read in reads[band]:
            read.wait()
        low, high = band * SUBLANES, min(columns, (band + 1) * SUBLANES)
        for out, half in ((other, 1 - core), (own, core)):
            for block in range(blocks):
                at = pl.ds(pl.multiple_of((2 * block + half) * LANES, LANES), LANES)
                tile = h_here[low:high, at] - POLE_SHIFT * s_here[low:high, at]
                if high - low < SUBLANES:
                    rest = jnp.zeros((SUBLANES - high + low, LANES), jnp.float32)
                    tile = jnp.concatenate([tile, rest])
                out[band * blocks + block] = tile
    live_read.wait()
    groups = pattern.shape[0]
    group = lax.broadcasted_iota(jnp.int32, (SUBLANES, LANES), 1) // (LANES // groups)
    live = jnp.zeros((SUBLANES, LANES), jnp.float32)
    for g in range(groups):
        live = jnp.where(group == g, (flags[g] > 0).astype(jnp.float32), live)
    own[2 * tiles] = live


def inverse_kernel(m, high, low, here, sems):
    reads = [
        pltpu.make_async_copy(m.at[:, b, :], here.at[:, pl.ds(b * LANES, LANES)], sems.at[b])
        for b in range(m.shape[1])
    ]
    for read in reads:
        read.start()
    for b, read in enumerate(reads):
        read.wait()
        at = slice(b * LANES, (b + 1) * LANES)
        high[:, at], low[:, at] = split(here[:, at])


def pivot_kernel(wides, index, dinv, high, low, high_t, low_t, picked):
    core, place = lax.axis_index("narrow"), place_of(lax.axis_index("wide"), wides)
    total, width = picked.shape
    deep = total // (2 * wides)
    lane = lax.broadcasted_iota(jnp.int32, (deep, width), 1)
    for k, offset in enumerate(offsets(wides)):
        chip = chip_at((place + offset + wides) % wides, wides)
        for j, part in enumerate((core, 1 - core)):
            rows = index[pl.ds(pl.multiple_of((2 * chip + part) * deep, SUBLANES), deep), :]
            at = (2 * k + j) * deep
            picked[at : at + deep, :] = (lane == rows).astype(jnp.float32)
    half = width // 2
    chosen = picked[...].astype(jnp.bfloat16)
    for piece, out, out_t in zip(split(dinv[...]), (high, low), (high_t, low_t)):
        rows = jnp.dot(chosen, piece, preferred_element_type=jnp.float32)
        out_t[...] = rows.T.astype(jnp.bfloat16)
        rows = rows.astype(jnp.bfloat16)

        @pl.when(core == 0)
        def _():
            out[...] = rows

        @pl.when(core != 0)
        def _():
            out[:, :half] = rows[:, half:]
            out[:, half:] = rows[:, :half]


def factor_kernel(wides, high_t, low_t, *refs):
    parts, out = refs[:wides], refs[wides]
    chip = lax.axis_index("wide")
    bands = (parts[0].shape[0] - 1) // wides
    rows = jnp.concatenate([p[band * wides + chip] for p in parts for band in range(bands)])
    rows = rows * parts[0][bands * wides][:1, :]
    out[...] = dot3((high_t[...], low_t[...]), split(rows), ((1,), (0,)))


def product_kernel(wides, d_high, d_low, m_high, m_low, *refs):
    parts, (keep, send, live, p_high, p_low) = refs[:wides], refs[wides:]
    place = place_of(lax.axis_index("wide"), wides)
    bands = (parts[0].shape[0] - 1) // wides
    for part, offset in zip(parts, offsets(wides)):
        chip = chip_at((place + offset + wides) % wides, wides)
        live[pl.ds(chip, 1), :] = part[bands * wides][:1, :]
    deep = bands * SUBLANES
    for block in range(wides):
        row = live[block : block + 1, :]
        at = slice(block * LANES, (block + 1) * LANES)
        for k, part in enumerate(parts):
            rows = jnp.concatenate([part[band * wides + block] for band in range(bands)]) * row
            high, low = split(rows)
            p_high[k * deep : (k + 1) * deep, at] = high
            p_low[k * deep : (k + 1) * deep, at] = low
    first = dot3((m_high[...], m_low[...]), (p_high[...], p_low[...]), ((1,), (1,)))
    both = dot3(split(first), (d_high[...], d_low[...]), ((1,), (0,)))
    half = both.shape[1] // 2
    keep[...] = both[:, :half]
    send[...] = both[:, half:]


def corner_kernel(keep, received, factor, factor_other, term):
    core = lax.axis_index("narrow")
    half = keep.shape[0] // 2
    value = None
    for from_here, part in ((factor, core), (factor_other, 1 - core)):
        at = pl.ds(pl.multiple_of(part * half, SUBLANES), half)
        more = dot3(split(from_here[...]), split(keep[at, :] + received[at, :]), ((1,), (0,)))
        value = more if value is None else value + more
    term[...] = value


def local(wides, h_panel, s_panel, col_index, pattern, dinv, ainv_cc):
    columns, rows_all = h_panel.shape
    rows_here, blocks, _, unit = ainv_cc.shape
    width = dinv.shape[0]
    deep = -(-columns // SUBLANES) * SUBLANES
    tiles = deep // SUBLANES * blocks
    total = 2 * wides * deep
    wide, narrow = lax.axis_index("wide"), lax.axis_index("narrow")
    swap = [(0, 1), (1, 0)]
    f32, bf16 = jnp.float32, jnp.bfloat16
    ring = [*range(0, wides, 2), *range(1, wides, 2)[::-1]]
    ahead = [(ring[i], ring[(i + 1) % wides]) for i in range(wides)]
    back = [(b, a) for a, b in ahead]
    leap = [(2 * ring[i] + core, 2 * ring[(i + step) % wides] + core) for i in range(wides) for core, step in ((0, 2), (1, -2))]

    own, other = call(
        prep_kernel,
        [((2 * tiles + 1, SUBLANES, LANES), f32), ((tiles, SUBLANES, LANES), f32)],
        [HBM] * 3,
        tuple(in_hbm(x) for x in (pattern, h_panel, s_panel)),
        2 * h_panel.size,
        [
            pltpu.SMEM(pattern.shape, jnp.int32),
            pltpu.VMEM(h_panel.shape, f32),
            pltpu.VMEM(h_panel.shape, f32),
            pltpu.SemaphoreType.DMA(()),
            pltpu.SemaphoreType.DMA((2, deep // SUBLANES)),
        ],
    )
    mine = lax.dynamic_update_slice(own, lax.ppermute(other, "narrow", swap), (tiles, 0, 0))

    parts = [mine]
    up = down = mine
    for step in range(1, (wides + 1) // 2):
        if wides % 2 == 0 and step == wides // 2 - 1:
            far = lax.ppermute(jnp.where(narrow == 0, up, down), ("wide", "narrow"), leap)
        up = lax.ppermute(up, "wide", ahead)
        down = lax.ppermute(down, "wide", back)
        parts += [up, down]
    if wides % 2 == 0:
        parts.append(far)

    m_high, m_low = call(
        inverse_kernel,
        [((rows_here, blocks * unit), bf16)] * 2,
        [HBM],
        (in_hbm(ainv_cc.reshape(rows_here, blocks, unit)),),
        4 * ainv_cc.size,
        [pltpu.VMEM((rows_here, blocks * unit), f32), pltpu.SemaphoreType.DMA((blocks,))],
    )
    index = jnp.pad(col_index.reshape(-1, columns), ((0, 0), (0, deep - columns))).reshape(-1, 1)
    d_high, d_low, d_high_t, d_low_t = call(
        functools.partial(pivot_kernel, wides),
        [((total, width), bf16)] * 2 + [((width, total), bf16)] * 2,
        [VMEM] * 2,
        (index, dinv),
        4 * total * width * width,
        [pltpu.VMEM((total, width), f32)],
    )
    factor = call(
        functools.partial(factor_kernel, wides),
        [((width, unit), f32)],
        [VMEM] * (2 + wides),
        (d_high_t, d_low_t, *parts),
        6 * total * width * unit,
    )[0]
    factor_other = lax.ppermute(factor, "narrow", swap)
    keep, send = call(
        functools.partial(product_kernel, wides),
        [((rows_here, width // 2), f32)] * 2,
        [VMEM] * (4 + wides),
        (d_high, d_low, m_high, m_low, *parts),
        6 * total * rows_here * (blocks * unit + width),
        [pltpu.VMEM((blocks, unit), f32)] + [pltpu.VMEM((total, blocks * unit), bf16)] * 2,
    )
    received = lax.ppermute(send, "narrow", swap)
    term = call(
        corner_kernel,
        [((width, width // 2), f32)],
        [VMEM] * 4,
        (keep, received, factor, factor_other),
        6 * width * width * rows_here,
    )[0]
    share = width // wides
    rest, near = term, 1
    while near < wides:
        mate = [(i, i ^ near) for i in range(wides)]
        pieces = rest.reshape(-1, 2, share, rest.shape[-1])
        side = (wide // near) % 2
        sent = lax.ppermute(lax.dynamic_index_in_dim(pieces, 1 - side, 1, False), "wide", mate)
        rest = (lax.dynamic_index_in_dim(pieces, side, 1, False) + sent).reshape(-1, rest.shape[-1])
        near *= 2
    corner = lax.dynamic_slice(dinv, (wide * share, narrow * (width // 2)), (share, width // 2))
    return -(keep + received), corner + rest


def solution(mesh):
    placed = (
        P(("pole", "wide", "narrow"), None),
        P(("pole", "wide", "narrow"), None),
        P("pole"),
        P(("pole", "wide", "narrow")),
        P("pole", None),
        P(("pole", "wide"), None, "narrow", None),
    )
    return jax.shard_map(
        functools.partial(local, mesh.shape["wide"]),
        mesh=mesh,
        in_specs=placed,
        out_specs=(P(("pole", "wide"), "narrow"), P(("pole", "wide"), "narrow")),
        check_vma=False,
    )
```
